1024 devices in a mesh: row: 64 (over x, z), col: 16 (over y, core).
Axes of the slice: x: 4, y: 8, z: 16, core: 2. Of those that a mesh axis runs over, the one named last changes fastest.
Arguments:
- out_grad: bfloat16 [4096, 4096], P('col', 'row'), may hold values from -0.09375 to 0.09375
- inputs: bfloat16 [4096, 4096], P('row', 'col'), may hold values from -6 to 6
- left_root: bfloat16 [4096, 4096], P('row'), may hold values from -2 to 3, as said below
- right_root: bfloat16 [4096, 4096], P(None, 'col'), may hold values from -2 to 3, as said below
- momentum: float32 [4096, 4096], P('row', 'col'), may hold values from -6 to 6
Outputs:
- momentum_new: float32 [4096, 4096], P('row', 'col')
- update: bfloat16 [4096, 4096], P('row', 'col')
The draws below stay inside these ranges and needn't reach their ends.
Inputs may be any that keep to these rules, and one draw needn't show every extreme that they name: `left_root`: symmetric. `right_root`: symmetric.
All inputs are finite; a program needn't handle non-finite values.
Results may differ from the reference program's by a relative error of at most 0.0057.
Values may be sent and summed in bfloat16 or wider, within the bound.
No kernel may reach another device: no remote copies, remote signals or barrier semaphores. Data moves between devices by JAX's collectives and lax.ppermute only.
A program may use at most 32 MiB of HBM per device.

```python
import jax
import jax.numpy as jnp
from jax import lax

DOUT = 4096
DIN = 4096
TOKENS = 4096


def root_like(key, order):
    first, second = jax.random.split(jax.random.fold_in(key, 17))
    diag_vals = jax.random.uniform(first, (order,), jnp.float32, 0.5, 2.0)
    noise = jax.random.normal(second, (order, order), jnp.float32)
    spread = (noise + noise.T) * (0.45 * order ** (-0.5))
    spread = jnp.clip(spread, -1.9, 1.9)
    eye = jnp.eye(order, dtype=jnp.float32)
    return (spread * (1.0 - eye) + eye * diag_vals[:, None]).astype(jnp.bfloat16)


def draw_left_root(key, part):
    return root_like(key, DOUT)


def draw_right_root(key, part):
    return root_like(jax.random.fold_in(key, 3), DIN)


def levels(own_key, extent, cuts, least, high):
    factor_of = 1.0
    for position, blocks in cuts:
        steps = jax.random.uniform(jax.random.fold_in(jax.random.fold_in(own_key, 6), position), (blocks,), jnp.float32, least / len(cuts), high / len(cuts))
        factor_of = factor_of * jnp.repeat(jnp.exp(steps), extent[position] // blocks).reshape((-1,) + (1,) * (len(extent) - 1 - position))
    return factor_of


def gaussian(own_key, shape, width, bound, pieces=(), kind=jnp.bfloat16):
    gain = levels(own_key, shape, pieces, -0.22, 0.18) if pieces else 1.0
    values = jax.random.normal(own_key, shape, jnp.float32) * width * gain
    return jnp.minimum(jnp.maximum(values, -bound), bound).astype(kind)


def setup_inputs(seed: int = 0) -> dict:
    key_list = jax.random.split(jax.random.key(seed), 6)
    return {
        "out_grad": gaussian(key_list[0], (TOKENS, DOUT), TOKENS ** -0.5, 0.09375, ((0, 16), (1, 64))),
        "inputs": gaussian(key_list[1], (TOKENS, DIN), 1.0, 6.0, ((0, 64), (1, 16))),
        "left_root": draw_left_root(jax.random.fold_in(key_list[5], 71), 0),
        "right_root": draw_right_root(jax.random.fold_in(key_list[5], 71), 0),
        "momentum": gaussian(key_list[4], (DOUT, DIN), 1.0, 6.0, ((0, 64), (1, 16)), jnp.float32),
    }


def reference(out_grad, inputs, left_root, right_root, momentum):
    grad = lax.dot_general(out_grad, inputs, (((0,), (0,)), ((), ())), preferred_element_type=jnp.float32).astype(jnp.bfloat16)
    first = jnp.dot(left_root, grad, preferred_element_type=jnp.float32).astype(jnp.bfloat16)
    shaped = jnp.dot(first, right_root, preferred_element_type=jnp.float32)
    momentum_new = 0.9 * momentum + shaped
    update = (0.25 * (0.9 * momentum_new + shaped)).astype(jnp.bfloat16)
    return momentum_new, update
```

```python
import jax
import jax.numpy as jnp
from jax import lax
from jax.sharding import Mesh
from jax.sharding import PartitionSpec as P

ROW = ("x", "z")
COL = "col"


def contract(a, b, da, db):
    return lax.dot_general(a, b, (((da,), (db,)), ((), ())), preferred_element_type=jnp.float32)


def summed_over_x(parts):
    parts = lax.all_to_all(parts.astype(jnp.bfloat16), "x", 0, 0)
    total = parts[0].astype(jnp.float32)
    for k in range(1, parts.shape[0]):
        total += parts[k].astype(jnp.float32)
    return total.astype(jnp.bfloat16)


def body(out_grad, inputs, left_root, right_root, momentum):
    nx, nz = lax.axis_size("x"), lax.axis_size("z")
    rows, order = left_root.shape
    cols = inputs.shape[1]
    wide = order // nx
    lows = nz // nx

    turn = []
    for x in range(nx):
        for high in range(lows):
            for low in range(nx):
                turn.append((x * nz + high * nx + low, low * nz + high * nx + x))
    turned = lax.ppermute(inputs, ROW, turn)

    left = lax.all_to_all(left_root.reshape(rows, nx, wide).transpose(1, 0, 2), "x", 0, 0)
    left = left.reshape(nx * rows, wide)

    tokens = lax.all_to_all(jnp.broadcast_to(turned, (nz, rows, cols)), "z", 0, 0)
    tokens = tokens.reshape(lows, nx, rows, cols).transpose(1, 0, 2, 3).reshape(-1, cols)

    cotangent = lax.all_gather(out_grad.T, "z", axis=0, tiled=True)
    part = contract(cotangent, left, 0, 1)
    product = summed_over_x(part.reshape(nx, rows, nx * rows))
    panel = lax.all_gather(product, COL, axis=0, tiled=True)

    part = contract(panel, tokens, 0, 0)
    first = summed_over_x(part.reshape(nx, rows, cols))
    panel = lax.all_gather(first, COL, axis=0)
    panel = panel.transpose(1, 0, 2).reshape(rows, -1)
    shaped = contract(panel, right_root, 1, 0)
    momentum_new = 0.9 * momentum + shaped
    update = (0.25 * (0.9 * momentum_new + shaped)).astype(jnp.bfloat16)
    return (momentum_new, update)


def solution(mesh):
    split = Mesh(mesh.devices.reshape(4, 16, mesh.shape["col"]), ("x", "z", "col"))
    in_specs = (P("col", ROW), P(ROW, "col"), P(ROW, None), P(None, "col"), P(ROW, "col"))
    out_specs = (P(ROW, "col"), P(ROW, "col"))
    return jax.shard_map(body, mesh=split, in_specs=in_specs, out_specs=out_specs, check_vma=False)
```

```python
import jax
import jax.numpy as jnp
from jax import lax
from jax.sharding import Mesh
from jax.sharding import PartitionSpec as P

ROW = ("x", "z")
COL = "col"


def contract(a, b, da, db):
    return lax.dot_general(a, b, (((da,), (db,)), ((), ())), preferred_element_type=jnp.float32)


def summed_over_x(parts):
    parts = lax.all_to_all(parts, "x", 0, 0)
    total = parts[0].astype(jnp.float32)
    for k in range(1, parts.shape[0]):
        total += parts[k].astype(jnp.float32)
    return total.astype(jnp.bfloat16)


def body(out_grad, inputs, left_root, right_root, momentum):
    nx, nz = lax.axis_size("x"), lax.axis_size("z")
    rows, order = left_root.shape
    cols = inputs.shape[1]
    wide = order // nx

    share = rows // nx
    half = share // 2
    rest = jnp.zeros((half, wide - 2 * cols), inputs.dtype)
    blocks = []
    for x in range(nx):
        own = inputs[x * share : (x + 1) * share]
        own = jnp.concatenate([own[:half], own[half:], rest], axis=1)
        blocks.append(jnp.concatenate([left_root[:, x * wide : (x + 1) * wide], own], axis=0))
    with jax.named_scope("turn"):
        got = lax.all_to_all(jnp.stack(blocks), "x", 0, 0)
    left = got[:, :rows].reshape(nx * rows, wide)
    own = got[:, rows:]
    own = jnp.stack([own[:, :, :cols], own[:, :, cols : 2 * cols]], axis=1)

    cotangent = lax.all_gather(out_grad.T, "z", axis=0, tiled=True)

    own = jnp.broadcast_to(own.reshape(rows, cols), (nz, rows, cols))
    with jax.named_scope("tokens"):
        tokens = lax.all_to_all(own, "z", 0, 0)
    tokens = tokens.reshape(nz, nx, share, cols).transpose(1, 0, 2, 3).reshape(-1, cols)

    part = contract(cotangent, left, 0, 1).astype(jnp.bfloat16)
    part = part.reshape(-1, nx, share, nx * rows).transpose(1, 0, 2, 3).reshape(nx, -1, nx * rows)
    with jax.named_scope("product"):
        product = summed_over_x(part)
    panel = lax.all_gather(product, COL, axis=0, tiled=True)

    part = contract(panel, tokens, 0, 0).astype(jnp.bfloat16).reshape(nx, rows, cols)
    first = summed_over_x(part)
    panel = lax.all_gather(first, COL, axis=0)
    panel = panel.transpose(1, 0, 2).reshape(rows, -1)
    shaped = contract(panel, right_root, 1, 0)
    momentum_new = 0.9 * momentum + shaped
    update = (0.25 * (0.9 * momentum_new + shaped)).astype(jnp.bfloat16)
    return (momentum_new, update)


def solution(mesh):
    split = Mesh(mesh.devices.reshape(4, 16, mesh.shape["col"]), ("x", "z", "col"))
    in_specs = (P("col", ROW), P(ROW, "col"), P(ROW, None), P(None, "col"), P(ROW, "col"))
    out_specs = (P(ROW, "col"), P(ROW, "col"))
    return jax.shard_map(body, mesh=split, in_specs=in_specs, out_specs=out_specs, check_vma=False)
```

```python
import jax
import jax.numpy as jnp
from jax import lax
from jax.experimental import pallas as pl
from jax.experimental.pallas import tpu as pltpu
from jax.sharding import Mesh
from jax.sharding import PartitionSpec as P

ROW = ("x", "z")
COL = "col"


def contract(a, b, da, db):
    return lax.dot_general(a, b, (((da,), (db,)), ((), ())), preferred_element_type=jnp.float32)


def summed_over_x(parts):
    parts = lax.all_to_all(parts, "x", 0, 0)
    total = parts[0].astype(jnp.float32)
    for k in range(1, parts.shape[0]):
        total += parts[k].astype(jnp.float32)
    return total.astype(jnp.bfloat16)


def pack(left_ref, own_ref, out_ref):
    rows = left_ref.shape[0]
    cols = own_ref.shape[1]
    out_ref[0, :rows] = left_ref[...]
    out_ref[0, rows:, :cols] = own_ref[...]
    out_ref[0, rows:, cols:] = jnp.zeros((own_ref.shape[0], out_ref.shape[2] - cols), out_ref.dtype)


def packed(left_root, inputs, n):
    rows, order = left_root.shape
    wide, share, cols = order // n, inputs.shape[0] // n, inputs.shape[1]
    return pl.pallas_call(
        pack,
        grid=(n,),
        in_specs=[pl.BlockSpec((rows, wide), lambda x: (0, x)), pl.BlockSpec((share, cols), lambda x: (x, 0))],
        out_specs=pl.BlockSpec((1, rows + share, wide), lambda x: (x, 0, 0)),
        out_shape=jax.ShapeDtypeStruct((n, rows + share, wide), left_root.dtype),
    )(left_root, inputs)


def body(out_grad, inputs, left_root, right_root, momentum):
    nx, nz = lax.axis_size("x"), lax.axis_size("z")
    rows, order = left_root.shape
    cols = inputs.shape[1]
    wide = order // nx
    share = rows // nx

    got = lax.all_to_all(packed(left_root, inputs, nx), "x", 0, 0)
    left = got[:, :rows].reshape(nx * rows, wide)

    cotangent = lax.all_gather(out_grad.T, "z", axis=0).reshape(wide, -1)

    own = jnp.broadcast_to(got[:, rows:, :cols].reshape(rows, cols), (nz, rows, cols))
    part = contract(cotangent, left, 0, 1).astype(jnp.bfloat16)
    part = part.reshape(-1, nx, share, nx * rows).transpose(1, 0, 2, 3).reshape(nx, -1, nx * rows)
    part, own = lax.optimization_barrier((part, own))
    product = summed_over_x(part)

    tokens = lax.all_to_all(own, "z", 0, 0)
    tokens = tokens.reshape(nz, nx, share, cols).transpose(1, 0, 2, 3).reshape(-1, cols)
    panel = lax.all_gather(product, COL, axis=0, tiled=True)

    part = contract(panel, tokens, 0, 0).astype(jnp.bfloat16).reshape(nx, rows, cols)
    first = summed_over_x(part)
    panel = lax.all_gather(first, COL, axis=0)
    panel = panel.transpose(1, 0, 2).reshape(rows, -1)
    shaped = contract(panel, right_root, 1, 0)
    momentum_new = 0.9 * momentum + shaped
    update = (0.25 * (0.9 * momentum_new + shaped)).astype(jnp.bfloat16)
    return (momentum_new, update)


def solution(mesh):
    split = Mesh(mesh.devices.reshape(4, 16, mesh.shape["col"]), ("x", "z", "col"))
    in_specs = (P("col", ROW), P(ROW, "col"), P(ROW, None), P(None, "col"), P(ROW, "col"))
    out_specs = (P(ROW, "col"), P(ROW, "col"))
    return jax.shard_map(body, mesh=split, in_specs=in_specs, out_specs=out_specs, check_vma=False)
```

```python
import jax
import jax.numpy as jnp
from jax import lax
from jax.experimental import pallas as pl
from jax.experimental.pallas import tpu as pltpu
from jax.sharding import Mesh
from jax.sharding import PartitionSpec as P


ROW = ("x", "z")
COL = "col"


def contract(a, b, da, db):
    return lax.dot_general(a, b, (((da,), (db,)), ((), ())), preferred_element_type=jnp.float32)


def summed_over_x(parts):
    parts = lax.all_to_all(parts, "x", 0, 0)
    total = parts[0].astype(jnp.float32)
    for k in range(1, parts.shape[0]):
        total += parts[k].astype(jnp.float32)
    return total.astype(jnp.bfloat16)


def summed_by_permutes(parts):
    n = parts.shape[0]
    me = lax.axis_index("x")
    total = lax.dynamic_index_in_dim(parts, me, 0, False).astype(jnp.float32)
    for k in range(1, n):
        sent = lax.dynamic_index_in_dim(parts, lax.rem(me + k, n), 0, False)
        total += lax.ppermute(sent, "x", [(x, (x + k) % n) for x in range(n)]).astype(jnp.float32)
    return total.astype(jnp.bfloat16)


def pack(left_ref, own_ref, out_ref, held, fetched, stored):
    n, _, wide = held.shape
    rows = left_ref.shape[0]
    share, cols = own_ref.shape[0] // n, own_ref.shape[1]
    fetches = []
    for x in range(n):
        for k, (source, target) in enumerate(
            (
                (left_ref.at[:, pl.ds(x * wide, wide)], held.at[x, pl.ds(0, rows)]),
                (own_ref.at[pl.ds(x * share, share)], held.at[x, pl.ds(rows, share), pl.ds(0, cols)]),
            )
        ):
            copy = pltpu.make_async_copy(source, target, fetched.at[x, k])
            copy.start()
            fetches.append(copy)
    held[:, rows:, cols:] = jnp.zeros((n, share, wide - cols), held.dtype)
    stores = []
    for x in range(n):
        fetches[2 * x].wait()
        fetches[2 * x + 1].wait()
        copy = pltpu.make_async_copy(held.at[x], out_ref.at[x], stored.at[x])
        copy.start()
        stores.append(copy)
    for copy in stores:
        copy.wait()


def packed(left_root, inputs, n):
    rows, order = left_root.shape
    shape = (n, rows + inputs.shape[0] // n, order // n)
    return pl.pallas_call(
        pack,
        in_specs=[pl.BlockSpec(memory_space=pl.ANY)] * 2,
        out_specs=pl.BlockSpec(memory_space=pl.ANY),
        out_shape=jax.ShapeDtypeStruct(shape, left_root.dtype),
        scratch_shapes=[
            pltpu.VMEM(shape, left_root.dtype),
            pltpu.SemaphoreType.DMA((n, 2)),
            pltpu.SemaphoreType.DMA((n,)),
        ],
    )(left_root, inputs)


def body(out_grad, inputs, left_root, right_root, momentum):
    nx, nz = lax.axis_size("x"), lax.axis_size("z")
    rows, order = left_root.shape
    cols = inputs.shape[1]
    wide = order // nx
    share = rows // nx

    blocks = packed(left_root, inputs, nx)
    got = lax.all_to_all(blocks, "x", 0, 0)
    left = got[:, :rows].reshape(nx * rows, wide)

    cotangent = lax.all_gather(out_grad.T, "z", axis=0, tiled=True)

    own = jnp.broadcast_to(got[:, rows:, :cols].reshape(rows, cols), (nz, rows, cols))
    part = contract(cotangent, left, 0, 1).astype(jnp.bfloat16)
    part = part.reshape(-1, nx, share, nx * rows).transpose(1, 0, 2, 3).reshape(nx, -1, nx * rows)
    product = summed_by_permutes(part)

    tokens = lax.all_to_all(own, "z", 0, 0)
    tokens = tokens.reshape(nz, nx, share, cols).transpose(1, 0, 2, 3).reshape(-1, cols)
    panel = lax.all_gather(product, COL, axis=0, tiled=True)

    part = contract(panel, tokens, 0, 0).astype(jnp.bfloat16).reshape(nx, rows, cols)
    first = summed_over_x(part)
    panel = lax.all_gather(first, COL, axis=0)
    panel = panel.transpose(1, 0, 2).reshape(rows, -1)
    shaped = contract(panel, right_root, 1, 0)
    momentum_new = 0.9 * momentum + shaped
    update = (0.25 * (0.9 * momentum_new + shaped)).astype(jnp.bfloat16)
    return (momentum_new, update)


def solution(mesh):
    split = Mesh(mesh.devices.reshape(4, 16, mesh.shape["col"]), ("x", "z", "col"))
    in_specs = (P("col", ROW), P(ROW, "col"), P(ROW, None), P(None, "col"), P(ROW, "col"))
    out_specs = (P(ROW, "col"), P(ROW, "col"))

    def step(*args):
        return body(*args)

    step = jax.shard_map(step, mesh=split, in_specs=in_specs, out_specs=out_specs, check_vma=False)
    return step
```

```python
import jax
import jax.numpy as jnp
from jax import lax
from jax.experimental import pallas as pl
from jax.experimental.pallas import tpu as pltpu
from jax.sharding import Mesh
from jax.sharding import PartitionSpec as P

ROW = ("x", "z")
COL = "col"


def contract(a, b, da, db):
    return lax.dot_general(a, b, (((da,), (db,)), ((), ())), preferred_element_type=jnp.float32)


def summed_over_x(parts):
    parts = lax.all_to_all(parts, "x", 0, 0)
    total = parts[0].astype(jnp.float32)
    for k in range(1, parts.shape[0]):
        total += parts[k].astype(jnp.float32)
    return total


def pack(place_ref, left_ref, own_ref, out_ref, held, fetched, stored):
    n, copies, both, cols = out_ref.shape
    share = both // 2
    wide = left_ref.shape[1] // n
    across = wide // cols
    down = pl.multiple_of(place_ref[0] // across * share, share)
    right = place_ref[0] % across * cols
    fetches = []
    for x in range(n):
        left = left_ref.at[pl.ds(down, share), pl.ds(pl.multiple_of(x * wide + right, cols), cols)]
        own = own_ref.at[pl.ds(x * share, share)]
        for k, source in enumerate((left, own)):
            copy = pltpu.make_async_copy(source, held.at[x, pl.ds(k * share, share)], fetched.at[x, k])
            copy.start()
            fetches.append(copy)
    stores = []
    for x in range(n):
        fetches[2 * x].wait()
        fetches[2 * x + 1].wait()
        for c in range(copies):
            copy = pltpu.make_async_copy(held.at[x], out_ref.at[x, c], stored.at[x, c])
            copy.start()
            stores.append(copy)
    for copy in stores:
        copy.wait()


def packed(left_root, inputs, n, copies):
    share, cols = inputs.shape[0] // n, inputs.shape[1]
    return pl.pallas_call(
        pack,
        in_specs=[
            pl.BlockSpec(memory_space=pltpu.SMEM),
            pl.BlockSpec(memory_space=pl.ANY),
            pl.BlockSpec(memory_space=pl.ANY),
        ],
        out_specs=pl.BlockSpec(memory_space=pl.ANY),
        out_shape=jax.ShapeDtypeStruct((n, copies, 2 * share, cols), inputs.dtype),
        scratch_shapes=[
            pltpu.VMEM((n, 2 * share, cols), inputs.dtype),
            pltpu.SemaphoreType.DMA((n, 2)),
            pltpu.SemaphoreType.DMA((n, copies)),
        ],
    )(lax.axis_index(COL).astype(jnp.int32)[None], left_root, inputs)


def body(out_grad, inputs, left_root, right_root, momentum):
    nx, nz, nc = lax.axis_size("x"), lax.axis_size("z"), lax.axis_size(COL)
    rows, order = left_root.shape
    cols = inputs.shape[1]
    wide = order // nx
    share = rows // nx

    blocks = packed(left_root, inputs, nx, nc).reshape(nx * nc, 2 * share, cols)
    with jax.named_scope("turn"):
        got = lax.all_to_all(blocks, ("x", COL), 0, 0)
    left = got[:, :share].reshape(nx, rows // share, wide // cols, share, cols)
    left = left.transpose(0, 1, 3, 2, 4).reshape(nx * rows, wide)
    own = got[:, share:].reshape(nx, nc, share, cols).transpose(0, 2, 1, 3).reshape(rows, -1)

    with jax.named_scope("cotangent"):
        cotangent = lax.all_gather(out_grad.T, "z", axis=0, tiled=True)

    part = contract(cotangent, left, 0, 1).astype(jnp.bfloat16)
    part = part.reshape(-1, nx, share, nx * rows).transpose(1, 0, 2, 3).reshape(nx, -1, nx * rows)
    product = summed_over_x(part).astype(jnp.bfloat16)

    own = contract(own, right_root, 1, 0).astype(jnp.bfloat16)
    own = jnp.broadcast_to(own, (nz, rows, cols))
    tokens = lax.all_to_all(own, "z", 0, 0)
    tokens = tokens.reshape(nz, nx, share, cols).transpose(1, 0, 2, 3).reshape(-1, cols)
    panel = lax.all_gather(product, COL, axis=0, tiled=True)

    part = contract(panel, tokens, 0, 0).astype(jnp.bfloat16).reshape(nx, rows, cols)
    shaped = summed_over_x(part)
    momentum_new = 0.9 * momentum + shaped
    update = (0.25 * (0.9 * momentum_new + shaped)).astype(jnp.bfloat16)
    return (momentum_new, update)


def solution(mesh):
    split = Mesh(mesh.devices.reshape(4, 16, mesh.shape["col"]), ("x", "z", "col"))
    in_specs = (P("col", ROW), P(ROW, "col"), P(ROW, None), P(None, "col"), P(ROW, "col"))
    out_specs = (P(ROW, "col"), P(ROW, "col"))
    return jax.shard_map(body, mesh=split, in_specs=in_specs, out_specs=out_specs, check_vma=False)
```

```python
import jax
import jax.numpy as jnp
from jax import lax
from jax.experimental import pallas as pl
from jax.experimental.pallas import tpu as pltpu
from jax.sharding import Mesh
from jax.sharding import PartitionSpec as P


ROW = ("x", "z")
COL = ("y", "core")


def contract(a, b, da, db):
    return lax.dot_general(a, b, (((da,), (db,)), ((), ())), preferred_element_type=jnp.float32)


def summed_over_x(parts):
    parts = lax.all_to_all(parts, "x", 0, 0)
    total = parts[0].astype(jnp.float32)
    for k in range(1, parts.shape[0]):
        total += parts[k].astype(jnp.float32)
    return total


def pack(place_ref, left_ref, own_ref, out_ref, held, fetched, stored):
    n, copies, both, cols = out_ref.shape
    share = own_ref.shape[0] // n
    piece = both - share
    wide = left_ref.shape[1] // n
    across = wide // cols
    down = pl.multiple_of(place_ref[0] // across * piece, piece)
    right = place_ref[0] % across * cols
    fetches = []
    for x in range(n):
        left = left_ref.at[pl.ds(down, piece), pl.ds(pl.multiple_of(x * wide + right, cols), cols)]
        own = own_ref.at[pl.ds(x * share, share)]
        for k, (source, start) in enumerate(((left, 0), (own, piece))):
            copy = pltpu.make_async_copy(source, held.at[x, pl.ds(start, source.shape[0])], fetched.at[x, k])
            copy.start()
            fetches.append(copy)
    stores = []
    for x in range(n):
        fetches[2 * x].wait()
        fetches[2 * x + 1].wait()
        for c in range(copies):
            copy = pltpu.make_async_copy(held.at[x], out_ref.at[x, c], stored.at[x, c])
            copy.start()
            stores.append(copy)
    for copy in stores:
        copy.wait()


def packed(left_root, inputs, n, copies):
    share, cols = inputs.shape[0] // n, inputs.shape[1]
    both = left_root.size // (n * copies * cols) + share
    return pl.pallas_call(
        pack,
        in_specs=[
            pl.BlockSpec(memory_space=pltpu.SMEM),
            pl.BlockSpec(memory_space=pl.ANY),
            pl.BlockSpec(memory_space=pl.ANY),
        ],
        out_specs=pl.BlockSpec(memory_space=pl.ANY),
        out_shape=jax.ShapeDtypeStruct((n, copies, both, cols), inputs.dtype),
        scratch_shapes=[
            pltpu.VMEM((n, both, cols), inputs.dtype),
            pltpu.SemaphoreType.DMA((n, 2)),
            pltpu.SemaphoreType.DMA((n, copies)),
        ],
    )(lax.axis_index("y").astype(jnp.int32)[None], left_root, inputs)


def body(out_grad, inputs, left_root, right_root, momentum):
    nx, nz, ny, nk = (lax.axis_size(name) for name in ("x", "z", "y", "core"))
    rows, order = left_root.shape
    cols = inputs.shape[1]
    wide = order // nx
    share = rows // nx
    piece = rows * wide // (ny * cols)

    blocks = packed(left_root, inputs, nx, ny).reshape(nx * ny, piece + share, cols)
    got = lax.all_to_all(blocks, ("x", "y"), 0, 0)
    left = got[:, :piece].reshape(nx, rows // piece, wide // cols, piece, cols)
    left = left.transpose(0, 1, 3, 2, 4).reshape(nx * rows, wide)

    cotangent = lax.all_gather(out_grad.T, "z", axis=0).reshape(wide, -1)

    part = contract(cotangent, left, 0, 1).astype(jnp.bfloat16)
    part = part.reshape(-1, nx, share, nx * rows).transpose(1, 0, 2, 3).reshape(nx, -1, nx * rows)
    part, own = lax.optimization_barrier((part, got[:, piece:].reshape(-1, cols)))
    product = summed_over_x(part).astype(jnp.bfloat16)

    own = lax.all_gather(own, "core", axis=0, tiled=True)
    own = own.reshape(nk, nx * ny, share, cols).transpose(1, 0, 2, 3)
    own = lax.optimization_barrier(own.reshape(nx, ny * nk, share, cols))
    own = own.transpose(0, 2, 1, 3).reshape(rows, -1)
    own = contract(own, right_root, 1, 0).astype(jnp.bfloat16)
    own = jnp.broadcast_to(own, (nz, rows, cols))
    tokens = lax.all_to_all(own, "z", 0, 0)
    tokens = tokens.reshape(nz, nx, share, cols).transpose(1, 0, 2, 3).reshape(-1, cols)
    panel = lax.all_gather(product, COL, axis=0, tiled=True)

    part = contract(panel, tokens, 0, 0).astype(jnp.bfloat16).reshape(nx, rows, cols)
    shaped = summed_over_x(part)
    momentum_new = 0.9 * momentum + shaped
    update = (0.25 * (0.9 * momentum_new + shaped)).astype(jnp.bfloat16)
    return (momentum_new, update)


def solution(mesh):
    split = Mesh(mesh.devices.reshape(4, 16, 8, 2), ("x", "z", "y", "core"))
    in_specs = (P(COL, ROW), P(ROW, COL), P(ROW, None), P(None, COL), P(ROW, COL))
    out_specs = (P(ROW, COL), P(ROW, COL))

    def step(*args):
        return body(*args)

    step = jax.shard_map(step, mesh=split, in_specs=in_specs, out_specs=out_specs, check_vma=False)
    return step
```

```python
import jax
import jax.numpy as jnp
from jax import lax
from jax.experimental import pallas as pl
from jax.experimental.pallas import tpu as pltpu
from jax.sharding import Mesh
from jax.sharding import PartitionSpec as P

ROW = ("x", "z")
COL = "col"


def contract(a, b, da, db):
    return lax.dot_general(a, b, (((da,), (db,)), ((), ())), preferred_element_type=jnp.float32)


def summed_over_x(parts):
    parts = lax.all_to_all(parts, "x", 0, 0)
    total = parts[0].astype(jnp.float32)
    for k in range(1, parts.shape[0]):
        total += parts[k].astype(jnp.float32)
    return total


def pack(place_ref, left_ref, own_ref, out_ref, held, fetched, stored):
    n, copies, both, cols = out_ref.shape
    share = both // 2
    wide = left_ref.shape[1] // n
    across = wide // cols
    down = pl.multiple_of(place_ref[0] // across * share, share)
    right = place_ref[0] % across * cols
    fetches = []
    for x in range(n):
        left = left_ref.at[pl.ds(down, share), pl.ds(pl.multiple_of(x * wide + right, cols), cols)]
        own = own_ref.at[pl.ds(x * share, share)]
        for k, source in enumerate((left, own)):
            copy = pltpu.make_async_copy(source, held.at[x, pl.ds(k * share, share)], fetched.at[x, k])
            copy.start()
            fetches.append(copy)
    stores = []
    for x in range(n):
        fetches[2 * x].wait()
        fetches[2 * x + 1].wait()
        for c in range(copies):
            copy = pltpu.make_async_copy(held.at[x], out_ref.at[x, c], stored.at[x, c])
            copy.start()
            stores.append(copy)
    for copy in stores:
        copy.wait()


def packed(left_root, inputs, n, copies):
    share, cols = inputs.shape[0] // n, inputs.shape[1]
    return pl.pallas_call(
        pack,
        in_specs=[
            pl.BlockSpec(memory_space=pltpu.SMEM),
            pl.BlockSpec(memory_space=pl.ANY),
            pl.BlockSpec(memory_space=pl.ANY),
        ],
        out_specs=pl.BlockSpec(memory_space=pl.ANY),
        out_shape=jax.ShapeDtypeStruct((n, copies, 2 * share, cols), inputs.dtype),
        scratch_shapes=[
            pltpu.VMEM((n, 2 * share, cols), inputs.dtype),
            pltpu.SemaphoreType.DMA((n, 2)),
            pltpu.SemaphoreType.DMA((n, copies)),
        ],
    )(lax.axis_index(COL).astype(jnp.int32)[None], left_root, inputs)


def body(out_grad, inputs, left_root, right_root, momentum):
    nx, nz, nc = lax.axis_size("x"), lax.axis_size("z"), lax.axis_size(COL)
    rows, order = left_root.shape
    cols = inputs.shape[1]
    wide = order // nx
    share = rows // nx

    blocks = packed(left_root, inputs, nx, nc).reshape(nx * nc, 2 * share, cols)
    with jax.named_scope("turn"):
        got = lax.all_to_all(blocks, ("x", COL), 0, 0)
    left = got[:, :share].reshape(nx, rows // share, wide // cols, share, cols)
    left = left.transpose(0, 1, 3, 2, 4).reshape(nx * rows, wide)

    with jax.named_scope("cotangent"):
        cotangent = lax.all_gather(out_grad.T, "z", axis=0).reshape(wide, -1)

    part = contract(cotangent, left, 0, 1).astype(jnp.bfloat16)
    part = part.reshape(-1, nx, share, nx * rows).transpose(1, 0, 2, 3).reshape(nx, -1, nx * rows)
    part, got = lax.optimization_barrier((part, got))
    own = got[:, share:].reshape(nx, nc, share, cols).transpose(0, 2, 1, 3).reshape(rows, -1)
    own = contract(own, right_root, 1, 0).astype(jnp.bfloat16)
    part, own = lax.optimization_barrier((part, jnp.broadcast_to(own, (nz, rows, cols))))
    product = summed_over_x(part).astype(jnp.bfloat16)

    tokens = lax.all_to_all(own, "z", 0, 0)
    tokens = tokens.reshape(nz, nx, share, cols).transpose(1, 0, 2, 3).reshape(-1, cols)
    panel = lax.all_gather(product, COL, axis=0, tiled=True)

    part = contract(panel, tokens, 0, 0).astype(jnp.bfloat16).reshape(nx, rows, cols)
    shaped = summed_over_x(part)
    momentum_new = 0.9 * momentum + shaped
    update = (0.25 * (0.9 * momentum_new + shaped)).astype(jnp.bfloat16)
    return (momentum_new, update)


def solution(mesh):
    split = Mesh(mesh.devices.reshape(4, 16, mesh.shape["col"]), ("x", "z", "col"))
    in_specs = (P("col", ROW), P(ROW, "col"), P(ROW, None), P(None, "col"), P(ROW, "col"))
    out_specs = (P(ROW, "col"), P(ROW, "col"))
    return jax.shard_map(body, mesh=split, in_specs=in_specs, out_specs=out_specs, check_vma=False)
```

```python
import jax
import jax.numpy as jnp
from jax import lax
from jax.experimental import pallas as pl
from jax.experimental.pallas import tpu as pltpu
from jax.sharding import Mesh
from jax.sharding import PartitionSpec as P

ROW = ("x", "z")
COL = "col"


def contract(a, b, da, db):
    return lax.dot_general(a, b, (((da,), (db,)), ((), ())), preferred_element_type=jnp.float32)


def summed_over_x(parts):
    parts = lax.all_to_all(parts, "x", 0, 0)
    total = parts[0].astype(jnp.float32)
    for k in range(1, parts.shape[0]):
        total += parts[k].astype(jnp.float32)
    return total


def pack(place_ref, left_ref, own_ref, out_ref, held, fetched, stored):
    n, copies, both, cols = out_ref.shape
    share = both // 2
    wide = left_ref.shape[1] // n
    across = wide // cols
    down = pl.multiple_of(place_ref[0] // across * share, share)
    right = place_ref[0] % across * cols
    fetches = []
    for x in range(n):
        left = left_ref.at[pl.ds(down, share), pl.ds(pl.multiple_of(x * wide + right, cols), cols)]
        own = own_ref.at[pl.ds(x * share, share)]
        for k, source in enumerate((left, own)):
            copy = pltpu.make_async_copy(source, held.at[x, pl.ds(k * share, share)], fetched.at[x, k])
            copy.start()
            fetches.append(copy)
    stores = []
    for x in range(n):
        fetches[2 * x].wait()
        fetches[2 * x + 1].wait()
        for c in range(copies):
            copy = pltpu.make_async_copy(held.at[x], out_ref.at[x, c], stored.at[x, c])
            copy.start()
            stores.append(copy)
    for copy in stores:
        copy.wait()


def packed(left_root, inputs, n, copies):
    share, cols = inputs.shape[0] // n, inputs.shape[1]
    return pl.pallas_call(
        pack,
        in_specs=[
            pl.BlockSpec(memory_space=pltpu.SMEM),
            pl.BlockSpec(memory_space=pl.ANY),
            pl.BlockSpec(memory_space=pl.ANY),
        ],
        out_specs=pl.BlockSpec(memory_space=pl.ANY),
        out_shape=jax.ShapeDtypeStruct((n, copies, 2 * share, cols), inputs.dtype),
        scratch_shapes=[
            pltpu.VMEM((n, 2 * share, cols), inputs.dtype),
            pltpu.SemaphoreType.DMA((n, 2)),
            pltpu.SemaphoreType.DMA((n, copies)),
        ],
    )(lax.axis_index(COL).astype(jnp.int32)[None], left_root, inputs)


def spread(got_ref, right_ref, out_ref, own, right, fetched):
    n, copies, share, cols = own.shape
    copy_own = pltpu.make_async_copy(got_ref.at[:, :, pl.ds(share, share)], own, fetched.at[copies])
    copy_own.start()
    fetches = []
    for c in range(copies):
        copy = pltpu.make_async_copy(right_ref.at[pl.ds(c * cols, cols)], right.at[c], fetched.at[c])
        copy.start()
        fetches.append(copy)
    copy_own.wait()
    total = jnp.zeros((n * share, cols), jnp.float32)
    for c in range(copies):
        fetches[c].wait()
        total += jnp.dot(own[:, c].reshape(n * share, cols), right[c], preferred_element_type=jnp.float32)
    out_ref[...] = jnp.broadcast_to(total.astype(out_ref.dtype), out_ref.shape)


def spread_product(got, right_root, copies):
    n, nc, both, cols = got.shape
    share = both // 2
    return pl.pallas_call(
        spread,
        in_specs=[pl.BlockSpec(memory_space=pl.ANY)] * 2,
        out_specs=pl.BlockSpec(memory_space=pltpu.VMEM),
        out_shape=jax.ShapeDtypeStruct((copies, n * share, cols), got.dtype),
        scratch_shapes=[
            pltpu.VMEM((n, nc, share, cols), got.dtype),
            pltpu.VMEM((nc, cols, cols), got.dtype),
            pltpu.SemaphoreType.DMA((nc + 1,)),
        ],
    )(got, right_root)


def body(out_grad, inputs, left_root, right_root, momentum):
    nx, nz, nc = lax.axis_size("x"), lax.axis_size("z"), lax.axis_size(COL)
    rows, order = left_root.shape
    cols = inputs.shape[1]
    wide = order // nx
    share = rows // nx

    blocks = packed(left_root, inputs, nx, nc).reshape(nx * nc, 2 * share, cols)
    with jax.named_scope("turn"):
        got = lax.all_to_all(blocks, ("x", COL), 0, 0)
    left = got[:, :share].reshape(nx, rows // share, wide // cols, share, cols)
    left = left.transpose(0, 1, 3, 2, 4).reshape(nx * rows, wide)

    with jax.named_scope("cotangent"):
        cotangent = lax.all_gather(out_grad.T, "z", axis=0).reshape(wide, -1)

    part = contract(cotangent, left, 0, 1).astype(jnp.bfloat16)
    part = part.reshape(-1, nx, share, nx * rows).transpose(1, 0, 2, 3).reshape(nx, -1, nx * rows)
    part, got = lax.optimization_barrier((part, got))
    own = spread_product(got.reshape(nx, nc, 2 * share, cols), right_root, nz)
    part, own = lax.optimization_barrier((part, own))
    product = summed_over_x(part).astype(jnp.bfloat16)

    tokens = lax.all_to_all(own, "z", 0, 0)
    tokens = tokens.reshape(nz, nx, share, cols).transpose(1, 0, 2, 3).reshape(-1, cols)
    panel = lax.all_gather(product, COL, axis=0, tiled=True)

    part = contract(panel, tokens, 0, 0).astype(jnp.bfloat16).reshape(nx, rows, cols)
    shaped = summed_over_x(part)
    momentum_new = 0.9 * momentum + shaped
    update = (0.25 * (0.9 * momentum_new + shaped)).astype(jnp.bfloat16)
    return (momentum_new, update)


def solution(mesh):
    split = Mesh(mesh.devices.reshape(4, 16, mesh.shape["col"]), ("x", "z", "col"))
    in_specs = (P("col", ROW), P(ROW, "col"), P(ROW, None), P(None, "col"), P(ROW, "col"))
    out_specs = (P(ROW, "col"), P(ROW, "col"))
    return jax.shard_map(body, mesh=split, in_specs=in_specs, out_specs=out_specs, check_vma=False)
```

```python
import jax
import jax.numpy as jnp
from jax import lax
from jax.experimental import pallas as pl
from jax.experimental.pallas import tpu as pltpu
from jax.sharding import Mesh
from jax.sharding import PartitionSpec as P


ROW = ("x", "z")
COL = "col"


def contract(a, b, da, db):
    return lax.dot_general(a, b, (((da,), (db,)), ((), ())), preferred_element_type=jnp.float32)


def summed_over_x(parts):
    parts = lax.all_to_all(parts, "x", 0, 0)
    total = parts[0].astype(jnp.float32)
    for k in range(1, parts.shape[0]):
        total += parts[k].astype(jnp.float32)
    return total


def pack(place_ref, left_ref, own_ref, out_ref, held, fetched, stored):
    n, copies, both, cols = out_ref.shape
    share = both // 2
    wide = left_ref.shape[1] // n
    across = wide // cols
    down = pl.multiple_of(place_ref[0] // across * share, share)
    right = place_ref[0] % across * cols
    fetches = []
    for x in range(n):
        left = left_ref.at[pl.ds(down, share), pl.ds(pl.multiple_of(x * wide + right, cols), cols)]
        own = own_ref.at[pl.ds(x * share, share)]
        for k, source in enumerate((left, own)):
            copy = pltpu.make_async_copy(source, held.at[x, pl.ds(k * share, share)], fetched.at[x, k])
            copy.start()
            fetches.append(copy)
    stores = []
    for x in range(n):
        fetches[2 * x].wait()
        fetches[2 * x + 1].wait()
        for c in range(copies):
            copy = pltpu.make_async_copy(held.at[x], out_ref.at[x, c], stored.at[x, c])
            copy.start()
            stores.append(copy)
    for copy in stores:
        copy.wait()


def packed(left_root, inputs, n, copies):
    share, cols = inputs.shape[0] // n, inputs.shape[1]
    return pl.pallas_call(
        pack,
        in_specs=[
            pl.BlockSpec(memory_space=pltpu.SMEM),
            pl.BlockSpec(memory_space=pl.ANY),
            pl.BlockSpec(memory_space=pl.ANY),
        ],
        out_specs=pl.BlockSpec(memory_space=pl.ANY),
        out_shape=jax.ShapeDtypeStruct((n, copies, 2 * share, cols), inputs.dtype),
        scratch_shapes=[
            pltpu.VMEM((n, 2 * share, cols), inputs.dtype),
            pltpu.SemaphoreType.DMA((n, 2)),
            pltpu.SemaphoreType.DMA((n, copies)),
        ],
    )(lax.axis_index(COL).astype(jnp.int32)[None], left_root, inputs)


def spread(got_ref, right_ref, out_ref, own, right, fetched):
    n, copies, share, cols = own.shape
    copy_own = pltpu.make_async_copy(got_ref.at[:, :, pl.ds(share, share)], own, fetched.at[copies])
    copy_own.start()
    fetches = []
    for c in range(copies):
        copy = pltpu.make_async_copy(right_ref.at[pl.ds(c * cols, cols)], right.at[c], fetched.at[c])
        copy.start()
        fetches.append(copy)
    copy_own.wait()
    total = jnp.zeros((n * share, cols), jnp.float32)
    for c in range(copies):
        fetches[c].wait()
        total += jnp.dot(own[:, c].reshape(n * share, cols), right[c], preferred_element_type=jnp.float32)
    out_ref[...] = jnp.broadcast_to(total.astype(out_ref.dtype), out_ref.shape)


def spread_product(got, right_root, copies):
    n, nc, both, cols = got.shape
    share = both // 2
    return pl.pallas_call(
        spread,
        in_specs=[pl.BlockSpec(memory_space=pl.ANY)] * 2,
        out_specs=pl.BlockSpec(memory_space=pltpu.VMEM),
        out_shape=jax.ShapeDtypeStruct((copies, n * share, cols), got.dtype),
        scratch_shapes=[
            pltpu.VMEM((n, nc, share, cols), got.dtype),
            pltpu.VMEM((nc, cols, cols), got.dtype),
            pltpu.SemaphoreType.DMA((nc + 1,)),
        ],
    )(got, right_root)


def body(out_grad, inputs, left_root, right_root, momentum):
    nx, nz, nc = lax.axis_size("x"), lax.axis_size("z"), lax.axis_size(COL)
    rows, order = left_root.shape
    cols = inputs.shape[1]
    wide = order // nx
    share = rows // nx

    blocks = packed(left_root, inputs, nx, nc).reshape(nx * nc, 2 * share, cols)
    got = lax.all_to_all(blocks, ("x", COL), 0, 0)
    left = got[:, :share].reshape(nx, rows // share, wide // cols, share, cols)
    left = left.transpose(0, 1, 3, 2, 4).reshape(nx * rows, wide)

    cotangent = lax.all_gather(out_grad.T, "z", axis=0).reshape(wide, -1)

    part = contract(cotangent, left, 0, 1).astype(jnp.bfloat16)
    part = part.reshape(-1, nx, share, nx * rows).transpose(1, 0, 2, 3).reshape(nx, -1, nx * rows)
    part, got = lax.optimization_barrier((part, got))
    product = summed_over_x(part).astype(jnp.bfloat16)
    own = spread_product(got.reshape(nx, nc, 2 * share, cols), right_root, nz)

    tokens = lax.all_to_all(own, "z", 0, 0)
    tokens = tokens.reshape(nz, nx, share, cols).transpose(1, 0, 2, 3).reshape(-1, cols)
    panel = lax.all_gather(product, COL, axis=0, tiled=True)

    part = contract(panel, tokens, 0, 0).astype(jnp.bfloat16).reshape(nx, rows, cols)
    shaped = summed_over_x(part)
    momentum_new = 0.9 * momentum + shaped
    update = (0.25 * (0.9 * momentum_new + shaped)).astype(jnp.bfloat16)
    return (momentum_new, update)


def solution(mesh):
    split = Mesh(mesh.devices.reshape(4, 16, mesh.shape["col"]), ("x", "z", "col"))
    in_specs = (P("col", ROW), P(ROW, "col"), P(ROW, None), P(None, "col"), P(ROW, "col"))
    out_specs = (P(ROW, "col"), P(ROW, "col"))

    def step(*args):
        return body(*args)

    step = jax.shard_map(step, mesh=split, in_specs=in_specs, out_specs=out_specs, check_vma=False)
    return step
```

```python
import jax
import jax.numpy as jnp
from jax import lax
from jax.experimental import pallas as pl
from jax.experimental.pallas import tpu as pltpu
from jax.sharding import Mesh
from jax.sharding import PartitionSpec as P


ROW = ("x", "z")
COL = "col"


def contract(a, b, da, db):
    return lax.dot_general(a, b, (((da,), (db,)), ((), ())), preferred_element_type=jnp.float32)


def summed_over_x(parts):
    parts = lax.all_to_all(parts, "x", 0, 0)
    total = parts[0].astype(jnp.float32)
    for k in range(1, parts.shape[0]):
        total += parts[k].astype(jnp.float32)
    return total


def pack(place_ref, left_ref, own_ref, out_ref, held, fetched, stored):
    n, copies, both, cols = out_ref.shape
    share = both // 2
    wide = left_ref.shape[1] // n
    across = wide // cols
    down = pl.multiple_of(place_ref[0] // across * share, share)
    right = place_ref[0] % across * cols
    fetches = []
    for x in range(n):
        left = left_ref.at[pl.ds(down, share), pl.ds(pl.multiple_of(x * wide + right, cols), cols)]
        own = own_ref.at[pl.ds(x * share, share)]
        for k, source in enumerate((left, own)):
            copy = pltpu.make_async_copy(source, held.at[x, pl.ds(k * share, share)], fetched.at[x, k])
            copy.start()
            fetches.append(copy)
    stores = []
    for x in range(n):
        fetches[2 * x].wait()
        fetches[2 * x + 1].wait()
        for c in range(copies):
            copy = pltpu.make_async_copy(held.at[x], out_ref.at[x, c], stored.at[x, c])
            copy.start()
            stores.append(copy)
    for copy in stores:
        copy.wait()


def packed(left_root, inputs, n, copies):
    share, cols = inputs.shape[0] // n, inputs.shape[1]
    return pl.pallas_call(
        pack,
        in_specs=[
            pl.BlockSpec(memory_space=pltpu.SMEM),
            pl.BlockSpec(memory_space=pl.ANY),
            pl.BlockSpec(memory_space=pl.ANY),
        ],
        out_specs=pl.BlockSpec(memory_space=pl.ANY),
        out_shape=jax.ShapeDtypeStruct((n, copies, 2 * share, cols), inputs.dtype),
        scratch_shapes=[
            pltpu.VMEM((n, 2 * share, cols), inputs.dtype),
            pltpu.SemaphoreType.DMA((n, 2)),
            pltpu.SemaphoreType.DMA((n, copies)),
        ],
    )(lax.axis_index(COL).astype(jnp.int32)[None], left_root, inputs)


def spread(got_ref, right_ref, out_ref, own, right, fetched):
    n, copies, share, cols = own.shape
    copy_own = pltpu.make_async_copy(got_ref.at[:, :, pl.ds(share, share)], own, fetched.at[copies])
    copy_own.start()
    fetches = []
    for c in range(copies):
        copy = pltpu.make_async_copy(right_ref.at[pl.ds(c * cols, cols)], right.at[c], fetched.at[c])
        copy.start()
        fetches.append(copy)
    copy_own.wait()
    total = jnp.zeros((n * share, cols), jnp.float32)
    for c in range(copies):
        fetches[c].wait()
        total += jnp.dot(own[:, c].reshape(n * share, cols), right[c], preferred_element_type=jnp.float32)
    out_ref[...] = jnp.broadcast_to(total.astype(out_ref.dtype), out_ref.shape)


def spread_product(got, right_root, copies):
    n, nc, both, cols = got.shape
    share = both // 2
    return pl.pallas_call(
        spread,
        in_specs=[pl.BlockSpec(memory_space=pl.ANY)] * 2,
        out_specs=pl.BlockSpec(memory_space=pltpu.VMEM),
        out_shape=jax.ShapeDtypeStruct((copies, n * share, cols), got.dtype),
        scratch_shapes=[
            pltpu.VMEM((n, nc, share, cols), got.dtype),
            pltpu.VMEM((nc, cols, cols), got.dtype),
            pltpu.SemaphoreType.DMA((nc + 1,)),
        ],
        compiler_params=pltpu.CompilerParams(vmem_limit_bytes=16 << 20),
    )(got, right_root)


def body(out_grad, inputs, left_root, right_root, momentum):
    nx, nz, nc = lax.axis_size("x"), lax.axis_size("z"), lax.axis_size(COL)
    rows, order = left_root.shape
    cols = inputs.shape[1]
    wide = order // nx
    share = rows // nx

    blocks = packed(left_root, inputs, nx, nc).reshape(nx * nc, 2 * share, cols)
    got = lax.all_to_all(blocks, ("x", COL), 0, 0)
    left = got[:, :share].reshape(nx, rows // share, wide // cols, share, cols)
    left = left.transpose(0, 1, 3, 2, 4).reshape(nx * rows, wide)

    cotangent = lax.all_gather(out_grad.T, "z", axis=0).reshape(wide, -1)

    part = contract(cotangent, left, 0, 1).astype(jnp.bfloat16)
    part = part.reshape(-1, nx, share, nx * rows).transpose(1, 0, 2, 3).reshape(nx, -1, nx * rows)
    part, got = lax.optimization_barrier((part, got))
    own = spread_product(got.reshape(nx, nc, 2 * share, cols), right_root, nz)
    tokens = lax.all_to_all(own, "z", 0, 0)
    tokens = tokens.reshape(nz, nx, share, cols).transpose(1, 0, 2, 3).reshape(-1, cols)

    parts = lax.all_gather(part.reshape(-1, nx * rows), "x", axis=0, tiled=True).reshape(nx, nx, -1, nx * rows)
    parts = lax.dynamic_index_in_dim(parts, lax.axis_index("x"), 1, False).astype(jnp.float32)
    product = (parts[0] + parts[1] if nx == 2 else parts[0] + parts[1] + parts[2] + parts[3]).astype(jnp.bfloat16)

    panel = lax.all_gather(product, COL, axis=0, tiled=True)

    part = contract(panel, tokens, 0, 0).astype(jnp.bfloat16).reshape(nx, rows, cols)
    shaped = summed_over_x(part)
    momentum_new = 0.9 * momentum + shaped
    update = (0.25 * (0.9 * momentum_new + shaped)).astype(jnp.bfloat16)
    return (momentum_new, update)


def solution(mesh):
    split = Mesh(mesh.devices.reshape(4, 16, mesh.shape["col"]), ("x", "z", "col"))
    in_specs = (P("col", ROW), P(ROW, "col"), P(ROW, None), P(None, "col"), P(ROW, "col"))
    out_specs = (P(ROW, "col"), P(ROW, "col"))

    def step(*args):
        return body(*args)

    step = jax.shard_map(step, mesh=split, in_specs=in_specs, out_specs=out_specs, check_vma=False)
    return step
```
